128 devices in a mesh: expert: 8 (over y, z_lo), shard: 16 (over z_hi, x, core).
Axes of the slice: x: 4, y: 4, z: 4 (z_hi: 2, z_lo: 2; z = z_hi * 2 + z_lo), core: 2. Of those that a mesh axis runs over, the one named last changes fastest.
Arguments:
- pre_hidden: bfloat16 [7680, 4096], P(('expert', 'shard')), may hold values from -12 to 12
- dec_resid: bfloat16 [16, 32, 4096], P('shard', 'expert'), may hold values from -12 to 12
- dec_query: bfloat16 [512, 4096], P('shard', 'expert'), may hold values from -4.5 to 4.5
- kv_pool: bfloat16 [8, 16896, 16, 256], P('expert', 'shard'), may hold values from -4.5 to 4.5
- page_table: int32 [16, 32, 128], P('shard'), may hold values from 0 to 1055, as said below
- cache_len: int32 [16, 32], P('shard'), may hold values from 2 to 2048, as said below
- out_weight: bfloat16 [4096, 4096], P('expert'), may hold values from -0.5 to 0.5
- norm_gain: float32 [4096], replicated, may hold values from 0.5 to 1.5
- route_ids_pre: int32 [7680, 2], P(('expert', 'shard')), may hold values from 0 to 7, as said below
- route_ids_dec: int32 [16, 32, 2], P('shard', 'expert'), may hold values from 0 to 7, as said below
- route_logit_pre: float32 [7680, 2], P(('expert', 'shard')), may hold values from -6 to 6
- route_logit_dec: float32 [16, 32, 2], P('shard', 'expert'), may hold values from -6 to 6
- expert_slot: int32 [8], replicated, may hold values from 0 to 7, each once
- w_gate: bfloat16 [8, 4096, 8192], P('expert', None, 'shard'), may hold values from -0.09375 to 0.09375
- w_up: bfloat16 [8, 4096, 8192], P('expert', None, 'shard'), may hold values from -0.09375 to 0.09375
- w_down: bfloat16 [8, 8192, 4096], P('expert', 'shard'), may hold values from -0.0625 to 0.0625
Outputs:
- mixed_pre: bfloat16 [7680, 4096], P(('expert', 'shard'))
- mixed_dec: bfloat16 [16, 32, 4096], P('shard', 'expert')
The draws below stay inside these ranges and needn't reach their ends.
Inputs may be any that keep to these rules, and one draw needn't show every extreme that they name: `cache_len`: the requests of one shard index hold at most 16384 cached positions together, and one of them holds exactly 2048. `page_table`: for request i of shard index s, entries j below ceil(cache_len[s, i] / 16) name pages of the pool of that shard index, all distinct over the shard index; the other entries are unused. `route_ids_pre`: each row names two different experts. The rows of one device (its 60 prefill rows and its 4 decode rows) name each expert at most 18 times, and some expert exactly 18 times on every device. `route_ids_dec`: as for route_ids_pre: a device's decode rows count with its prefill rows.
All inputs are finite; a program needn't handle non-finite values.
Results may differ from the reference program's by a relative error of at most 0.015.
Values may be sent and summed in bfloat16 or wider, within the bound.
A program may use at most 192 MiB of HBM per device.

```python
import jax
import jax.numpy as jnp
import numpy as np
from jax import lax

D = 4096
QH = 32
KVH = 8
HD = 128
EXPERTS = 8
FF = 8192
PAGE = 16
MAXLEN = 2048
PRE_DEV = 60
DEC_DEV = 32
GROUP = 4
FF_DEV = 512
CAP = 18
PRE = 7680
DEC = 512
CTX_DEV = 16384
POOL_DEV = 1056
MAXP = 128
N_EXPERT = 8
N_SHARD = 16
DEVICES = 128


def stream_drawn(key, shape):
    return jnp.clip(jax.random.normal(key, shape, jnp.float32), -4.0, 4.0)


def draw_pre_hidden(key, part):
    shape = (PRE_DEV * N_EXPERT * N_SHARD, D)
    values = stream_drawn(key, shape)
    return values.astype(jnp.bfloat16)


def draw_dec_resid(key, part):
    shape = (N_SHARD, DEC_DEV, D)
    values = stream_drawn(key, shape)
    return values.astype(jnp.bfloat16)


def layout(key):

    def per_shard(shard_key):
        key_long, key_weight, key_perm, key_focus = jax.random.split(shard_key, 4)
        longest = jax.random.randint(key_long, (), 0, DEC_DEV)
        draws = jax.random.randint(key_weight, (DEC_DEV,), 0, 33).astype(jnp.int32)
        weights = 1 + draws * draws * draws
        spare = CTX_DEV - MAXLEN - 2 * (DEC_DEV - 1)
        lengths = 2 + jnp.minimum(spare * weights // jnp.sum(weights), MAXLEN - 2)
        lengths = jnp.where(jnp.arange(DEC_DEV) == longest, MAXLEN, lengths).astype(jnp.int32)
        pages_used = (lengths + PAGE - 1) // PAGE
        offsets = jnp.cumsum(pages_used) - pages_used
        shuffled = jax.random.permutation(key_perm, POOL_DEV).astype(jnp.int32)
        entries = (offsets[:, None] + jnp.arange(MAXP, dtype=jnp.int32)[None, :]) % POOL_DEV
        page_rows = shuffled[entries].astype(jnp.int32)
        focus = jax.random.randint(key_focus, (), 0, DEC_DEV).astype(jnp.int32)
        return (lengths, page_rows, focus)
    shard_keys = jax.random.split(jax.random.fold_in(key, 7), N_SHARD)
    return jax.vmap(per_shard)(shard_keys)


def draw_cache_len(key, part):
    return layout(key)[0]


def draw_page_table(key, part):
    return layout(key)[1]


def draw_kv_pool(key, part):
    shape = (KVH, POOL_DEV * N_SHARD, PAGE, 2 * HD)
    base_key = jax.random.fold_in(key, 21)
    values = jnp.clip(jax.random.normal(base_key, shape, jnp.float32), -4.0, 4.0)
    return values.astype(jnp.bfloat16)


def draw_dec_query(key, part):
    shape = (DEC_DEV * N_SHARD, QH * HD)
    base_key = jax.random.fold_in(key, 23)
    values = jnp.clip(jax.random.normal(base_key, shape, jnp.float32), -4.0, 4.0)
    return values.astype(jnp.bfloat16)


def routes(key):
    rows_dev = PRE_DEV + DEC_DEV // N_EXPERT
    slot_cap = (rows_dev + 3) // 4 + 2
    others_n = EXPERTS - 1
    n_other = 2 * rows_dev - slot_cap
    pairs = n_other // 2
    cumul = [n_other * step // others_n for step in range(others_n + 1)]
    counts = [cumul[step + 1] - cumul[step] for step in range(others_n)]
    order_index = jnp.asarray(np.repeat(np.arange(others_n), counts).astype(np.int32))
    hot_expert = jax.random.randint(jax.random.fold_in(key, 31), (), 0, EXPERTS).astype(jnp.int32)

    def per_device(device_key):
        key_perm, key_flip, key_rows = jax.random.split(device_key, 3)
        others = (hot_expert + 1 + jax.random.permutation(key_perm, others_n).astype(jnp.int32)) % EXPERTS
        sequence = others[order_index]
        first_half = sequence[:pairs]
        second_half = sequence[pairs:]
        two_rows = jnp.stack([first_half[:rows_dev - slot_cap], second_half[:rows_dev - slot_cap]], axis=-1)
        singles = jnp.concatenate([first_half[rows_dev - slot_cap:], second_half[rows_dev - slot_cap:]])
        hot_rows = jnp.stack([jnp.full((slot_cap,), hot_expert, jnp.int32), singles], axis=-1)
        route_rows = jnp.concatenate([two_rows, hot_rows], axis=0)
        flips = jax.random.randint(key_flip, (rows_dev,), 0, 2)
        route_rows = jnp.where(flips[:, None] == 1, route_rows[:, ::-1], route_rows)
        shuffled = jax.random.permutation(key_rows, rows_dev).astype(jnp.int32)
        return route_rows[shuffled].astype(jnp.int32)
    device_keys = jax.random.split(jax.random.fold_in(key, 33), N_EXPERT * N_SHARD)
    return jax.vmap(per_device)(device_keys)


def draw_route_ids_pre(key, part):
    return routes(key)[:, :PRE_DEV].reshape(-1, 2)


def draw_route_ids_dec(key, part):
    dec_rows = DEC_DEV // N_EXPERT
    decode_part = routes(key)[:, PRE_DEV:].reshape(N_EXPERT, N_SHARD, dec_rows, 2)
    return jnp.transpose(decode_part, (1, 0, 2, 3)).reshape(N_SHARD, DEC_DEV, 2)


def levels(own_key, dims, shards, least, largest):
    level = 1.0
    for axis_at, shards_of in shards:
        heights = jax.random.uniform(jax.random.fold_in(jax.random.fold_in(own_key, 6), axis_at), (shards_of,), jnp.float32, least / len(shards), largest / len(shards))
        level = level * jnp.repeat(jnp.exp(heights), dims[axis_at] // shards_of).reshape((-1,) + (1,) * (len(dims) - 1 - axis_at))
    return level


def scatter_about(stream_key, dims, spread, limit, pieces=(), kind=jnp.bfloat16):
    result = spread * jax.random.normal(stream_key, dims, jnp.float32)
    if pieces:
        result = result * levels(stream_key, dims, pieces, -0.22, 0.18)
    return jnp.clip(result, -limit, limit).astype(kind)


def setup_inputs(seed: int = 0) -> dict:
    key_of = jax.random.split(jax.random.key(seed), 17)
    pre_hidden = draw_pre_hidden(jax.random.fold_in(key_of[16], 71), 0)
    dec_resid = draw_dec_resid(jax.random.fold_in(key_of[16], 71), 0)
    dec_query = draw_dec_query(jax.random.fold_in(key_of[16], 71), 0)
    kv_pool = draw_kv_pool(jax.random.fold_in(key_of[16], 71), 0)
    page_table = draw_page_table(jax.random.fold_in(key_of[16], 71), 0)
    cache_len = draw_cache_len(jax.random.fold_in(key_of[16], 71), 0)
    out_weight = scatter_about(key_of[6], (QH * HD, D), HD ** -0.5, 0.5, ((0, 8),))
    norm_gain = jnp.clip(jax.random.uniform(key_of[7], (D,), jnp.float32, 0.5, 1.5), 0.5, 1.5)
    route_ids_pre = draw_route_ids_pre(jax.random.fold_in(key_of[16], 71), 0)
    route_ids_dec = draw_route_ids_dec(jax.random.fold_in(key_of[16], 71), 0)
    route_logit_pre = scatter_about(key_of[10], (PRE, 2), 1.0, 6.0, ((0, 128),), jnp.float32)
    route_logit_dec = scatter_about(key_of[11], (N_SHARD, DEC_DEV, 2), 1.0, 6.0, ((0, 16), (1, 8)), jnp.float32)
    expert_slot = jax.random.permutation(key_of[12], EXPERTS).astype(jnp.int32)
    w_gate = scatter_about(key_of[13], (EXPERTS, D, FF), D ** -0.5, 0.09375, ((0, 8), (2, 16)))
    w_up = scatter_about(key_of[14], (EXPERTS, D, FF), D ** -0.5, 0.09375, ((0, 8), (2, 16)))
    w_down = scatter_about(key_of[15], (EXPERTS, FF, D), FF ** -0.5, 0.0625, ((0, 8), (1, 16)))
    return dict(pre_hidden=pre_hidden, dec_resid=dec_resid, dec_query=dec_query, kv_pool=kv_pool, page_table=page_table, cache_len=cache_len, out_weight=out_weight, norm_gain=norm_gain, route_ids_pre=route_ids_pre, route_ids_dec=route_ids_dec, route_logit_pre=route_logit_pre, route_logit_dec=route_logit_dec, expert_slot=expert_slot, w_gate=w_gate, w_up=w_up, w_down=w_down)


def attend_shard(shard_at, dec_query, kv_pool, page_table, cache_len):
    pool_part = lax.dynamic_slice_in_dim(kv_pool, shard_at * POOL_DEV, POOL_DEV, 1)
    page_rows = lax.dynamic_index_in_dim(page_table, shard_at, 0, keepdims=False)
    lengths = lax.dynamic_index_in_dim(cache_len, shard_at, 0, keepdims=False)
    queries = lax.dynamic_slice_in_dim(dec_query, shard_at * DEC_DEV, DEC_DEV, 0)
    queries = queries.reshape(DEC_DEV, KVH, GROUP, HD).astype(jnp.float32)
    gathered = pool_part[:, page_rows].reshape(KVH, DEC_DEV, MAXLEN, 2 * HD)
    key_cache = gathered[..., :HD].astype(jnp.float32)
    value_cache = gathered[..., HD:].astype(jnp.float32)
    scores = jnp.einsum('rkgd,krtd->rkgt', queries, key_cache) * HD ** (-0.5)
    live_pos = (jnp.arange(MAXLEN, dtype=jnp.int32)[None, :] < lengths[:, None])[:, None, None, :]
    row_top = lax.optimization_barrier(jnp.max(jnp.where(live_pos, scores, -jnp.inf), axis=-1, keepdims=True))
    weights_f = jnp.where(live_pos, jnp.exp(scores - row_top), 0.0)
    totals = lax.optimization_barrier(jnp.sum(weights_f, axis=-1))
    weights_b = lax.optimization_barrier(weights_f.astype(jnp.bfloat16)).astype(jnp.float32)
    summed = jnp.einsum('rkgt,krtd->rkgd', weights_b, value_cache)
    return (summed / totals[..., None]).astype(jnp.bfloat16).reshape(DEC_DEV, QH * HD)

def expert_rows(x_rows, gate_w, up_w, down_w):
    gate = jnp.dot(x_rows, gate_w, preferred_element_type=jnp.float32)
    upper = jnp.dot(x_rows, up_w, preferred_element_type=jnp.float32)
    act = (jax.nn.silu(gate) * upper).astype(jnp.bfloat16)

    def add_block(block_at, summed):
        act_part = lax.dynamic_slice_in_dim(act, block_at * FF_DEV, FF_DEV, 1)
        down_part = lax.dynamic_slice_in_dim(down_w, block_at * FF_DEV, FF_DEV, 0)
        term = jnp.dot(act_part, down_part, preferred_element_type=jnp.float32).astype(jnp.bfloat16)
        return summed + lax.optimization_barrier(term).astype(jnp.float32)
    summed = lax.fori_loop(0, N_SHARD, add_block, jnp.zeros((x_rows.shape[0], D), jnp.float32))
    return lax.optimization_barrier(summed.astype(jnp.bfloat16)).astype(jnp.float32)

def reference(pre_hidden, dec_resid, dec_query, kv_pool, page_table, cache_len, out_weight, norm_gain, route_ids_pre, route_ids_dec, route_logit_pre, route_logit_dec, expert_slot, w_gate, w_up, w_down):

    def attend_one(shard_at):
        return attend_shard(shard_at, dec_query, kv_pool, page_table, cache_len)
    attn = lax.map(attend_one, jnp.arange(N_SHARD, dtype=jnp.int32)).reshape(DEC, QH * HD)
    head_total = jnp.dot(attn, out_weight, preferred_element_type=jnp.float32)
    h_dec = (dec_resid.reshape(DEC, D).astype(jnp.float32) + head_total).astype(jnp.bfloat16)
    hidden = jnp.concatenate([pre_hidden, h_dec], axis=0)
    route_ids = jnp.concatenate([route_ids_pre, route_ids_dec.reshape(DEC, 2)], axis=0)
    logits = jnp.concatenate([route_logit_pre, route_logit_dec.reshape(DEC, 2)], axis=0)
    stream = hidden.astype(jnp.float32)
    normed = (stream * lax.rsqrt(lax.optimization_barrier(jnp.mean(stream * stream, axis=-1, keepdims=True)) + 1e-05) * norm_gain).astype(jnp.bfloat16)
    shares = jnp.stack([jax.nn.sigmoid(logits[:, 0] - logits[:, 1]), jax.nn.sigmoid(logits[:, 1] - logits[:, 0])], axis=-1)
    slot_of = jnp.zeros((EXPERTS,), jnp.int32).at[expert_slot].set(jnp.arange(EXPERTS, dtype=jnp.int32))
    bound = DEVICES * CAP
    combined = stream
    for expert in range(EXPERTS):
        picks = route_ids == expert
        named = jnp.any(picks, axis=1)
        share_here = lax.optimization_barrier(jnp.sum(jnp.where(picks, shares, 0.0), axis=1))
        chosen = jnp.nonzero(named, size=bound, fill_value=0)[0].astype(jnp.int32)
        valid = jnp.arange(bound, dtype=jnp.int32) < jnp.sum(named.astype(jnp.int32))
        slot_here = slot_of[expert]
        outputs = expert_rows(normed[chosen], w_gate[slot_here], w_up[slot_here], w_down[slot_here])
        weight_rows = jnp.where(valid, share_here[chosen], 0.0)
        combined = combined.at[chosen].add(weight_rows[:, None] * outputs)
    mixed_pre = combined[:PRE].astype(jnp.bfloat16)
    mixed_dec = combined[PRE:].astype(jnp.bfloat16).reshape(N_SHARD, DEC_DEV, D)
    return (mixed_pre, mixed_dec)
```

```python
import jax
import jax.numpy as jnp
from jax import lax
from jax.experimental import pallas as pl
from jax.experimental.pallas import tpu as pltpu
from jax.sharding import PartitionSpec as P

MESH = pl.DeviceIdType.MESH
X_CHIPS = 4
CORES = 2
Z_HALVES = 2
SHARD_PLANE = X_CHIPS * CORES
LOWEST = -1e30


def attention_kernel(q_ref, count_ref, kv_ref, out_ref, top, total, summed):
    step = pl.program_id(0)

    @pl.when(step == 0)
    def _():
        top[...] = jnp.full(top.shape, LOWEST, jnp.float32)
        total[...] = jnp.zeros(total.shape, jnp.float32)
        summed[...] = jnp.zeros(summed.shape, jnp.float32)

    head_dim = q_ref.shape[1]
    positions = kv_ref.shape[0]
    pages = count_ref.shape[2]
    page_size = positions // pages
    scores = lax.dot_general(
        q_ref[...], kv_ref[:, :head_dim], (((1,), (1,)), ((), ())), preferred_element_type=jnp.float32
    ) * head_dim ** (-0.5)
    page_of = lax.broadcasted_iota(jnp.int32, (pages, positions), 1) // page_size
    spread = (page_of == lax.broadcasted_iota(jnp.int32, (pages, positions), 0)).astype(jnp.bfloat16)
    counts = jnp.dot(count_ref[0], spread, preferred_element_type=jnp.float32)
    offset = (lax.broadcasted_iota(jnp.int32, (1, positions), 1) % page_size).astype(jnp.float32)
    live = counts > offset
    scores = jnp.where(live, scores, LOWEST)
    new_top = jnp.maximum(top[...], jnp.max(scores, axis=1, keepdims=True))
    scale = jnp.exp(top[...] - new_top)
    weights = jnp.where(live, jnp.exp(scores - new_top), 0.0)
    top[...] = new_top
    total[...] = total[...] * scale + jnp.sum(weights, axis=1, keepdims=True)
    summed[...] = summed[...] * scale + jnp.dot(
        weights.astype(jnp.bfloat16), kv_ref[:, head_dim:], preferred_element_type=jnp.float32
    )

    @pl.when(step == pl.num_programs(0) - 1)
    def _():
        out_ref[...] = (summed[...] / total[...]).astype(out_ref.dtype)


def pool_attention(dec_query, kv_pool, page_rows, lengths):
    dec_dev, local_cols = dec_query.shape
    _, pool_dev, page_size, twice_dim = kv_pool.shape
    head_dim = twice_dim // 2
    group = local_cols // head_dim
    max_pages = page_rows.shape[1]
    steps = 16
    pages = pool_dev // steps
    in_page = jnp.clip(
        lengths[:, None] - page_size * jnp.arange(max_pages, dtype=jnp.int32)[None, :], 0, page_size
    )
    pool_ids = jnp.arange(pool_dev, dtype=jnp.int32)
    counts = jnp.sum(
        jnp.where(page_rows[:, :, None] == pool_ids[None, None, :], in_page[:, :, None], 0), axis=1
    ).astype(jnp.bfloat16)
    counts = jnp.repeat(counts, group, axis=0).reshape(dec_dev * group, steps, pages).transpose(1, 0, 2)
    rows = dec_dev * group
    return pl.pallas_call(
        attention_kernel,
        grid=(steps,),
        in_specs=[
            pl.BlockSpec((rows, head_dim), lambda i: (0, 0)),
            pl.BlockSpec((1, rows, pages), lambda i: (i, 0, 0)),
            pl.BlockSpec((pages * page_size, twice_dim), lambda i: (i, 0)),
        ],
        out_specs=pl.BlockSpec((rows, head_dim), lambda i: (0, 0)),
        out_shape=jax.ShapeDtypeStruct((rows, head_dim), jnp.bfloat16),
        scratch_shapes=[
            pltpu.VMEM((rows, 1), jnp.float32),
            pltpu.VMEM((rows, 1), jnp.float32),
            pltpu.VMEM((rows, head_dim), jnp.float32),
        ],
        cost_estimate=pl.CostEstimate(
            flops=4 * rows * head_dim * pool_dev * page_size,
            bytes_accessed=pool_dev * page_size * twice_dim * 2,
            transcendentals=rows * pool_dev * page_size,
        ),
        name="pool_attention",
    )(dec_query.reshape(rows, head_dim), counts, kv_pool.reshape(pool_dev * page_size, twice_dim)).reshape(
        dec_dev, local_cols
    )


def plane_kernel(per_half, n_expert, src_ref, dst_ref, send_sem, recv_sem, own_sem):
    expert = lax.axis_index("expert")
    shard = lax.axis_index("shard")
    half, rest = shard // SHARD_PLANE, shard % SHARD_PLANE
    mine = half * n_expert + expert

    def peer(step):
        to_expert = (expert + step % n_expert) % n_expert
        to_half = (half + step // n_expert) % Z_HALVES
        return to_expert, to_half

    peers = Z_HALVES * n_expert
    barrier = pltpu.get_barrier_semaphore()
    for step in range(1, peers):
        to_expert, to_half = peer(step)
        pl.semaphore_signal(
            barrier, inc=1, device_id=(to_expert, to_half * SHARD_PLANE + rest), device_id_type=MESH
        )
    pl.semaphore_wait(barrier, peers - 1)
    copies = []
    for step in range(1, peers):
        to_expert, to_half = peer(step)
        block = to_half * n_expert + to_expert if per_half else to_expert
        copy = pltpu.make_async_remote_copy(
            src_ref=src_ref.at[block],
            dst_ref=dst_ref.at[mine],
            send_sem=send_sem.at[step],
            recv_sem=recv_sem.at[step],
            device_id=(to_expert, to_half * SHARD_PLANE + rest),
            device_id_type=MESH,
        )
        copy.start()
        copies.append(copy)
    own = pltpu.make_async_copy(src_ref.at[mine if per_half else expert], dst_ref.at[mine], own_sem)
    own.start()
    own.wait()
    for copy in copies:
        copy.wait()


def plane_exchange(blocks, n_expert, per_half, collective_id):
    peers = Z_HALVES * n_expert
    block = blocks.shape[1:]

    def kernel(*refs):
        plane_kernel(per_half, n_expert, *refs)

    return pl.pallas_call(
        kernel,
        out_shape=jax.ShapeDtypeStruct((peers,) + block, blocks.dtype),
        in_specs=[pl.BlockSpec(memory_space=pl.ANY)],
        out_specs=pl.BlockSpec(memory_space=pl.ANY),
        scratch_shapes=[
            pltpu.SemaphoreType.DMA((peers,)),
            pltpu.SemaphoreType.DMA((peers,)),
            pltpu.SemaphoreType.DMA,
        ],
        compiler_params=pltpu.CompilerParams(collective_id=collective_id, has_side_effects=True),
        name="plane_return" if per_half else "plane_send",
    )(blocks)


def expert_kernel(
    rows_ref, gate0, gate1, up0, up1, down0, down1, out_ref,
    held, partial, direct, relayed, act, gate, up, down,
    send_sem, recv_sem, load_sem,
):
    expert = lax.axis_index("expert")
    shard = lax.axis_index("shard")
    half, rest = shard // SHARD_PLANE, shard % SHARD_PLANE
    chip, core = rest // CORES, rest % CORES
    right = half * SHARD_PLANE + (chip + 1) % X_CHIPS * CORES + core
    left = half * SHARD_PLANE + (chip + X_CHIPS - 1) % X_CHIPS * CORES + core
    count = rows_ref.shape[0]
    part = count // 2
    low, high = pl.ds(0, part), pl.ds(part, part)

    loads = []
    for at, (src, dst) in enumerate(
        ((gate0, gate.at[0]), (up0, up.at[0]), (gate1, gate.at[1]), (up1, up.at[1]), (down0, down.at[0]), (down1, down.at[1]))
    ):
        load = pltpu.make_async_copy(src, dst, load_sem.at[at])
        load.start()
        loads.append(load)

    barrier = pltpu.get_barrier_semaphore()
    for neighbour in (left, right):
        pl.semaphore_signal(barrier, inc=1, device_id=(expert, neighbour), device_id_type=MESH)
    pl.semaphore_wait(barrier, 2)

    def send(at, src, dst, to):
        copy = pltpu.make_async_remote_copy(
            src_ref=src,
            dst_ref=dst,
            send_sem=send_sem.at[at],
            recv_sem=recv_sem.at[at],
            device_id=(expert, to),
            device_id_type=MESH,
        )
        copy.start()
        return copy

    first_r = send(0, rows_ref.at[low], held.at[0, low], right)
    first_l = send(1, rows_ref.at[high], held.at[0, high], left)
    second_r = send(2, rows_ref.at[high], held.at[1, high], right)
    second_l = send(3, rows_ref.at[low], held.at[1, low], left)
    for load in loads:
        load.wait()

    width = rows_ref.shape[1]
    ff = gate.shape[2]
    tile = 256
    wide = 512

    def feed_forward(src, dst):
        for side in range(2):
            @pl.loop(0, ff // tile)
            def _(t):
                columns = pl.ds(pl.multiple_of(t * tile, tile), tile)
                g = jnp.dot(src[...], gate[side, :, columns], preferred_element_type=jnp.float32)
                u = jnp.dot(src[...], up[side, :, columns], preferred_element_type=jnp.float32)
                act[side, :, columns] = (g / (1.0 + jnp.exp(-g)) * u).astype(act.dtype)

        @pl.loop(0, width // wide)
        def _(t):
            columns = pl.ds(pl.multiple_of(t * wide, wide), wide)
            o = jnp.dot(act[0], down[0, :, columns], preferred_element_type=jnp.float32)
            o = o + jnp.dot(act[1], down[1, :, columns], preferred_element_type=jnp.float32)
            dst[:, columns] = o.astype(dst.dtype)

    feed_forward(rows_ref, partial.at[3])
    first_r.wait_recv()
    third_r = send(4, held.at[0, low], held.at[2, low], right)
    first_l.wait_recv()
    third_l = send(5, held.at[0, high], held.at[2, high], left)
    feed_forward(held.at[0], partial.at[0])
    plain_r = send(6, partial.at[0, high], direct.at[0, high], right)
    plain_l = send(7, partial.at[0, low], direct.at[1, low], left)
    second_r.wait_recv()
    second_l.wait_recv()
    feed_forward(held.at[1], partial.at[1])
    third_r.wait_recv()
    third_l.wait_recv()
    feed_forward(held.at[2], partial.at[2])
    far_r = send(8, partial.at[2, low], relayed.at[low], right)
    far_l = send(9, partial.at[2, high], relayed.at[high], left)

    strip = 48

    def add_relayed(start):
        @pl.loop(0, part // strip)
        def _(t):
            lines = pl.ds(pl.multiple_of(start + t * strip, 16), strip)
            partial[1, lines, :] = (
                partial[1, lines, :].astype(jnp.float32) + relayed[lines, :].astype(jnp.float32)
            ).astype(partial.dtype)

    far_r.wait_recv()
    add_relayed(0)
    joined_r = send(10, partial.at[1, low], direct.at[0, low], right)
    far_l.wait_recv()
    add_relayed(part)
    joined_l = send(11, partial.at[1, high], direct.at[1, high], left)
    plain_r.wait_recv()
    plain_l.wait_recv()
    joined_r.wait_recv()
    joined_l.wait_recv()

    @pl.loop(0, count // strip)
    def _(t):
        lines = pl.ds(pl.multiple_of(t * strip, 16), strip)
        out_ref[lines, :] = (
            partial[3, lines, :].astype(jnp.float32)
            + direct[0, lines, :].astype(jnp.float32)
            + direct[1, lines, :].astype(jnp.float32)
        ).astype(out_ref.dtype)

    for copy in (
        first_r, first_l, second_r, second_l, third_r, third_l,
        plain_r, plain_l, far_r, far_l, joined_r, joined_l,
    ):
        copy.wait_send()


def expert_exchange(rows, gates, ups, downs, collective_id):
    count, width = rows.shape
    ff = gates[0].shape[1]
    bf16 = jnp.bfloat16
    vmem = pl.BlockSpec(memory_space=pltpu.VMEM)
    anywhere = pl.BlockSpec(memory_space=pl.ANY)
    return pl.pallas_call(
        expert_kernel,
        out_shape=jax.ShapeDtypeStruct((count, width), bf16),
        in_specs=[vmem] + [anywhere] * 6,
        out_specs=vmem,
        scratch_shapes=[
            pltpu.VMEM((3, count, width), bf16),
            pltpu.VMEM((4, count, width), bf16),
            pltpu.VMEM((2, count, width), bf16),
            pltpu.VMEM((count, width), bf16),
            pltpu.VMEM((2, count, ff), bf16),
            pltpu.VMEM((2, width, ff), bf16),
            pltpu.VMEM((2, width, ff), bf16),
            pltpu.VMEM((2, ff, width), bf16),
            pltpu.SemaphoreType.DMA((12,)),
            pltpu.SemaphoreType.DMA((12,)),
            pltpu.SemaphoreType.DMA((6,)),
        ],
        compiler_params=pltpu.CompilerParams(
            collective_id=collective_id, has_side_effects=True, vmem_limit_bytes=66 * 1024 * 1000 - 560000
        ),
        name="expert_exchange",
    )(rows, *gates, *ups, *downs)


def local(
    pre_hidden,
    dec_resid,
    dec_query,
    kv_pool,
    page_table,
    cache_len,
    out_weight,
    norm_gain,
    route_ids_pre,
    route_ids_dec,
    route_logit_pre,
    route_logit_dec,
    expert_slot,
    w_gate,
    w_up,
    w_down,
):
    n_expert = lax.axis_size("expert")
    n_shard = lax.axis_size("shard")
    swap = [(at, at ^ 1) for at in range(n_shard)]
    gates = (w_gate[0], lax.ppermute(w_gate[0], "shard", swap))
    ups = (w_up[0], lax.ppermute(w_up[0], "shard", swap))
    downs = (w_down[0], lax.ppermute(w_down[0], "shard", swap))
    attn = pool_attention(dec_query, kv_pool, page_table[0], cache_len[0])
    head_part = jnp.dot(attn, out_weight, preferred_element_type=jnp.float32).astype(jnp.bfloat16)
    head_parts = lax.all_to_all(
        head_part.reshape(n_expert, -1, head_part.shape[1]), "expert", split_axis=0, concat_axis=0, tiled=True
    )
    head_total = jnp.sum(head_parts.astype(jnp.float32), axis=0)
    h_dec = (dec_resid[0].astype(jnp.float32) + head_total).astype(jnp.bfloat16)
    hidden = jnp.concatenate([pre_hidden, h_dec], axis=0)
    route_ids = jnp.concatenate([route_ids_pre, route_ids_dec[0]], axis=0)
    logits = jnp.concatenate([route_logit_pre, route_logit_dec[0]], axis=0)
    pre_count = pre_hidden.shape[0]
    rows_dev, width = hidden.shape
    slot_cap = (rows_dev + 3) // 4 + 2
    stream = hidden.astype(jnp.float32)
    normed = (
        stream * lax.rsqrt(jnp.mean(stream * stream, axis=-1, keepdims=True) + 1e-05) * norm_gain
    ).astype(jnp.bfloat16)
    shares = jnp.stack(
        [jax.nn.sigmoid(logits[:, 0] - logits[:, 1]), jax.nn.sigmoid(logits[:, 1] - logits[:, 0])],
        axis=-1,
    )
    experts = expert_slot.shape[0]
    expert_ids = jnp.arange(experts, dtype=jnp.int32)
    slot_match = expert_slot[None, :] == expert_ids[:, None]
    slot_of = jnp.sum(jnp.where(slot_match, expert_ids[None, :], 0), axis=1)
    slot_ids = jnp.sum(jnp.where(route_ids[..., None] == expert_ids, slot_of, 0), axis=-1)
    flat_slots = slot_ids.reshape(-1)
    slot_hot = (flat_slots[:, None] == expert_ids[None, :]).astype(jnp.int32)
    ranking = jnp.sum((jnp.cumsum(slot_hot, axis=0) - slot_hot) * slot_hot, axis=1)
    slot_pos = (flat_slots * slot_cap + ranking).reshape(rows_dev, 2)
    slots_all = experts * slot_cap
    chosen = jnp.arange(slots_all, dtype=jnp.int32)[:, None, None] == slot_pos[None]
    placing = jnp.any(chosen, axis=-1).astype(jnp.bfloat16)
    buffer = jnp.dot(placing, normed, preferred_element_type=jnp.float32).astype(jnp.bfloat16)
    lanes = 128
    buffer = buffer.reshape(experts, slot_cap, width // lanes, lanes)
    received = plane_exchange(buffer, n_expert, False, 0)
    rows = received.reshape(-1, width)
    sums = expert_exchange(rows, gates, ups, downs, 1)
    returned = plane_exchange(
        sums.reshape(Z_HALVES * n_expert, slot_cap, width // lanes, lanes), n_expert, True, 2
    ).reshape(Z_HALVES, slots_all, width)
    outputs = (returned[0].astype(jnp.float32) + returned[1].astype(jnp.float32)).astype(jnp.bfloat16)
    picking = (slot_pos.T.reshape(-1)[:, None] == jnp.arange(slots_all, dtype=jnp.int32)[None, :]).astype(
        jnp.bfloat16
    )
    picked = jnp.dot(picking, outputs, preferred_element_type=jnp.float32).reshape(2, rows_dev, width)
    mixed_rows = stream + shares[:, :1] * picked[0] + shares[:, 1:] * picked[1]
    mixed_out = mixed_rows.astype(jnp.bfloat16)
    return (mixed_out[:pre_count], mixed_out[pre_count:][None])


def solution(mesh):
    placed = (
        P(("expert", "shard"), None),
        P("shard", "expert", None),
        P("shard", "expert"),
        P("expert", "shard", None, None),
        P("shard", None, None),
        P("shard", None),
        P("expert", None),
        P(),
        P(("expert", "shard"), None),
        P("shard", "expert", None),
        P(("expert", "shard"), None),
        P("shard", "expert", None),
        P(),
        P("expert", None, "shard"),
        P("expert", None, "shard"),
        P("expert", "shard", None),
    )
    return jax.shard_map(
        local,
        mesh=mesh,
        in_specs=placed,
        out_specs=(P(("expert", "shard"), None), P("shard", "expert", None)),
        check_vma=False,
    )
```

```python
import jax
import jax.numpy as jnp
from jax import lax
from jax.experimental import pallas as pl
from jax.experimental.pallas import tpu as pltpu
from jax.sharding import PartitionSpec as P

MESH = pl.DeviceIdType.MESH
X_CHIPS = 4
CORES = 2
Z_HALVES = 2
SHARD_PLANE = X_CHIPS * CORES
LOWEST = -1e30
BLOCK = 16
CHUNKS = 3


def attention_kernel(q_ref, count_ref, kv_ref, out_ref, top, total, summed):
    step = pl.program_id(0)

    @pl.when(step == 0)
    def _():
        top[...] = jnp.full(top.shape, LOWEST, jnp.float32)
        total[...] = jnp.zeros(total.shape, jnp.float32)
        summed[...] = jnp.zeros(summed.shape, jnp.float32)

    head_dim = q_ref.shape[1]
    positions = kv_ref.shape[0]
    pages = count_ref.shape[2]
    page_size = positions // pages
    scores = lax.dot_general(
        q_ref[...], kv_ref[:, :head_dim], (((1,), (1,)), ((), ())), preferred_element_type=jnp.float32
    ) * head_dim ** (-0.5)
    page_of = lax.broadcasted_iota(jnp.int32, (pages, positions), 1) // page_size
    spread = (page_of == lax.broadcasted_iota(jnp.int32, (pages, positions), 0)).astype(jnp.bfloat16)
    counts = jnp.dot(count_ref[0], spread, preferred_element_type=jnp.float32)
    offset = (lax.broadcasted_iota(jnp.int32, (1, positions), 1) % page_size).astype(jnp.float32)
    live = counts > offset
    scores = jnp.where(live, scores, LOWEST)
    new_top = jnp.maximum(top[...], jnp.max(scores, axis=1, keepdims=True))
    scale = jnp.exp(top[...] - new_top)
    weights = jnp.where(live, jnp.exp(scores - new_top), 0.0)
    top[...] = new_top
    total[...] = total[...] * scale + jnp.sum(weights, axis=1, keepdims=True)
    summed[...] = summed[...] * scale + jnp.dot(
        weights.astype(jnp.bfloat16), kv_ref[:, head_dim:], preferred_element_type=jnp.float32
    )

    @pl.when(step == pl.num_programs(0) - 1)
    def _():
        out_ref[...] = (summed[...] / total[...]).astype(out_ref.dtype)


def pool_attention(dec_query, kv_pool, page_rows, lengths):
    dec_dev, local_cols = dec_query.shape
    _, pool_dev, page_size, twice_dim = kv_pool.shape
    head_dim = twice_dim // 2
    group = local_cols // head_dim
    max_pages = page_rows.shape[1]
    steps = 16
    pages = pool_dev // steps
    in_page = jnp.clip(
        lengths[:, None] - page_size * jnp.arange(max_pages, dtype=jnp.int32)[None, :], 0, page_size
    )
    pool_ids = jnp.arange(pool_dev, dtype=jnp.int32)
    counts = jnp.sum(
        jnp.where(page_rows[:, :, None] == pool_ids[None, None, :], in_page[:, :, None], 0), axis=1
    ).astype(jnp.bfloat16)
    counts = jnp.repeat(counts, group, axis=0).reshape(dec_dev * group, steps, pages).transpose(1, 0, 2)
    rows = dec_dev * group
    return pl.pallas_call(
        attention_kernel,
        grid=(steps,),
        in_specs=[
            pl.BlockSpec((rows, head_dim), lambda i: (0, 0)),
            pl.BlockSpec((1, rows, pages), lambda i: (i, 0, 0)),
            pl.BlockSpec((pages * page_size, twice_dim), lambda i: (i, 0)),
        ],
        out_specs=pl.BlockSpec((rows, head_dim), lambda i: (0, 0)),
        out_shape=jax.ShapeDtypeStruct((rows, head_dim), jnp.bfloat16),
        scratch_shapes=[
            pltpu.VMEM((rows, 1), jnp.float32),
            pltpu.VMEM((rows, 1), jnp.float32),
            pltpu.VMEM((rows, head_dim), jnp.float32),
        ],
        cost_estimate=pl.CostEstimate(
            flops=4 * rows * head_dim * pool_dev * page_size,
            bytes_accessed=pool_dev * page_size * twice_dim * 2,
            transcendentals=rows * pool_dev * page_size,
        ),
        name="pool_attention",
    )(dec_query.reshape(rows, head_dim), counts, kv_pool.reshape(pool_dev * page_size, twice_dim)).reshape(
        dec_dev, local_cols
    )


def plane_kernel(per_half, n_expert, src_ref, dst_ref, send_sem, recv_sem, own_sem):
    expert = lax.axis_index("expert")
    shard = lax.axis_index("shard")
    half, rest = shard // SHARD_PLANE, shard % SHARD_PLANE
    mine = half * n_expert + expert

    def peer(step):
        to_expert = (expert + step % n_expert) % n_expert
        to_half = (half + step // n_expert) % Z_HALVES
        return to_expert, to_half

    peers = Z_HALVES * n_expert
    barrier = pltpu.get_barrier_semaphore()
    for step in range(1, peers):
        to_expert, to_half = peer(step)
        pl.semaphore_signal(
            barrier, inc=1, device_id=(to_expert, to_half * SHARD_PLANE + rest), device_id_type=MESH
        )
    pl.semaphore_wait(barrier, peers - 1)
    copies = []
    for step in range(1, peers):
        to_expert, to_half = peer(step)
        block = to_half * n_expert + to_expert if per_half else to_expert
        copy = pltpu.make_async_remote_copy(
            src_ref=src_ref.at[block],
            dst_ref=dst_ref.at[mine],
            send_sem=send_sem.at[step],
            recv_sem=recv_sem.at[step],
            device_id=(to_expert, to_half * SHARD_PLANE + rest),
            device_id_type=MESH,
        )
        copy.start()
        copies.append(copy)
    own = pltpu.make_async_copy(src_ref.at[mine if per_half else expert], dst_ref.at[mine], own_sem)
    own.start()
    own.wait()
    for copy in copies:
        copy.wait()


def plane_exchange(blocks, n_expert, per_half, collective_id):
    peers = Z_HALVES * n_expert
    block = blocks.shape[1:]

    def kernel(*refs):
        plane_kernel(per_half, n_expert, *refs)

    return pl.pallas_call(
        kernel,
        out_shape=jax.ShapeDtypeStruct((peers,) + block, blocks.dtype),
        in_specs=[pl.BlockSpec(memory_space=pl.ANY)],
        out_specs=pl.BlockSpec(memory_space=pl.ANY),
        scratch_shapes=[
            pltpu.SemaphoreType.DMA((peers,)),
            pltpu.SemaphoreType.DMA((peers,)),
            pltpu.SemaphoreType.DMA,
        ],
        compiler_params=pltpu.CompilerParams(collective_id=collective_id, has_side_effects=True),
        name="plane_return" if per_half else "plane_send",
    )(blocks)


def expert_kernel(
    blocks_ref, rest_ref, gate0, gate1, up0, up1, down0, down1, back_ref, rest_out,
    rows, held, partial, direct, relayed, sums, act, gate, up, down,
    plane_send, plane_recv, back_send, back_recv, send_sem, recv_sem, load_sem,
):
    expert = lax.axis_index("expert")
    shard = lax.axis_index("shard")
    n_expert, block, width = blocks_ref.shape
    half, rest = shard // SHARD_PLANE, shard % SHARD_PLANE
    chip, core = rest // CORES, rest % CORES
    right = half * SHARD_PLANE + (chip + 1) % X_CHIPS * CORES + core
    left = half * SHARD_PLANE + (chip + X_CHIPS - 1) % X_CHIPS * CORES + core
    mine = half * n_expert + expert
    peers = Z_HALVES * n_expert
    count = rows.shape[0]
    part = count // 2
    chunk = part // CHUNKS
    main = n_expert * block

    def ahead(step):
        to_half = (half + step // n_expert) % Z_HALVES
        return (expert + step) % n_expert, to_half * SHARD_PLANE + rest

    def behind(step):
        to_half = (half + step // n_expert) % Z_HALVES
        return (expert + n_expert - step % n_expert) % n_expert, to_half * SHARD_PLANE + rest

    def lines_of(step):
        return pl.ds(step // n_expert * part + step % n_expert * block, block)

    def local_copy(at, src, dst):
        copy = pltpu.make_async_copy(src, dst, load_sem.at[at])
        copy.start()
        return copy

    own = local_copy(6, blocks_ref.at[expert], rows.at[lines_of(0)])
    rests = [
        local_copy(7 + side, rest_ref.at[pl.ds(side * block, block)], rows.at[pl.ds(side * part + main, block)])
        for side in range(2)
    ]
    loads = [
        local_copy(at, src, dst)
        for at, (src, dst) in enumerate(
            ((gate0, gate.at[0]), (up0, up.at[0]), (gate1, gate.at[1]), (up1, up.at[1]), (down0, down.at[0]), (down1, down.at[1]))
        )
    ]

    barrier = pltpu.get_barrier_semaphore()
    for neighbour in (left, right):
        pl.semaphore_signal(barrier, inc=1, device_id=(expert, neighbour), device_id_type=MESH)
    for step in range(1, peers):
        pl.semaphore_signal(barrier, inc=1, device_id=ahead(step), device_id_type=MESH)
    pl.semaphore_wait(barrier, peers + 1)

    spread = []
    for step in range(1, peers):
        copy = pltpu.make_async_remote_copy(
            src_ref=blocks_ref.at[ahead(step)[0]],
            dst_ref=rows.at[lines_of(step)],
            send_sem=plane_send.at[step],
            recv_sem=plane_recv.at[step],
            device_id=ahead(step),
            device_id_type=MESH,
        )
        copy.start()
        spread.append(copy)

    sent = []

    def send(src, dst, to):
        at = len(sent)
        copy = pltpu.make_async_remote_copy(
            src_ref=src,
            dst_ref=dst,
            send_sem=send_sem.at[at],
            recv_sem=recv_sem.at[at],
            device_id=(expert, to),
            device_id_type=MESH,
        )
        copy.start()
        sent.append(copy)
        return copy

    near = [[], []]
    later = []

    def forward(lines, side):
        near[side].append(send(rows.at[lines], held.at[side, lines], right))
        later.append(send(rows.at[lines], held.at[1 - side, lines], left))

    for side in range(2):
        rests[side].wait()
        forward(pl.ds(side * part + main, block), side)
    own.wait()
    forward(lines_of(0), 0)
    for step in range(1, peers):
        spread[step - 1].wait_recv()
        forward(lines_of(step), step // n_expert)
    for load in loads:
        load.wait()

    ff = gate.shape[2]
    tile = 256
    wide = 512

    def feed_forward(src, dst):
        for side in range(2):
            @pl.loop(0, ff // tile)
            def _(t):
                columns = pl.ds(pl.multiple_of(t * tile, tile), tile)
                g = jnp.dot(src[...], gate[side, :, columns], preferred_element_type=jnp.float32)
                u = jnp.dot(src[...], up[side, :, columns], preferred_element_type=jnp.float32)
                act[side, :, columns] = (g / (1.0 + jnp.exp(-g)) * u).astype(act.dtype)

        @pl.loop(0, width // wide)
        def _(t):
            columns = pl.ds(pl.multiple_of(t * wide, wide), wide)
            o = jnp.dot(act[0], down[0, :, columns], preferred_element_type=jnp.float32)
            o = o + jnp.dot(act[1], down[1, :, columns], preferred_element_type=jnp.float32)
            dst[:, columns] = o.astype(dst.dtype)

    def piece(side, c):
        return pl.ds(side * part + c * chunk, chunk)

    feed_forward(rows, partial.at[3])
    for copy in near[0] + near[1] + later:
        copy.wait_recv()
    third = []
    for c in range(CHUNKS):
        third.append(send(held.at[0, piece(0, c)], held.at[2, piece(0, c)], right))
        third.append(send(held.at[0, piece(1, c)], held.at[2, piece(1, c)], left))
    feed_forward(held.at[0], partial.at[0])

    def send_plain(c):
        return (
            send(partial.at[0, piece(1, c)], direct.at[0, piece(1, c)], right),
            send(partial.at[0, piece(0, c)], direct.at[1, piece(0, c)], left),
        )

    def send_far(c):
        return (
            send(partial.at[2, piece(0, c)], relayed.at[piece(0, c)], right),
            send(partial.at[2, piece(1, c)], relayed.at[piece(1, c)], left),
        )

    def send_joined(c, far):
        joined = []
        for side, to in ((0, right), (1, left)):
            far[side].wait_recv()
            lines = piece(side, c)
            partial[1, lines, :] = (
                partial[1, lines, :].astype(jnp.float32) + relayed[lines, :].astype(jnp.float32)
            ).astype(partial.dtype)
            joined.append(send(partial.at[1, lines], direct.at[side, lines], to))
        return joined

    plain = [send_plain(0), send_plain(1)]
    feed_forward(held.at[1], partial.at[1])
    for copy in third:
        copy.wait_recv()
    feed_forward(held.at[2], partial.at[2])
    far = [send_far(0), send_far(1)]
    joined = [send_joined(0, far[0])]
    far.append(send_far(2))
    joined.append(send_joined(1, far[1]))
    plain.append(send_plain(2))
    joined.append(send_joined(2, far[2]))

    returns = []
    locals_ = []
    for c in range(CHUNKS):
        for copy in (*plain[c], *joined[c]):
            copy.wait_recv()
        for side in range(2):
            lines = piece(side, c)
            sums[lines, :] = (
                partial[3, lines, :].astype(jnp.float32)
                + direct[0, lines, :].astype(jnp.float32)
                + direct[1, lines, :].astype(jnp.float32)
            ).astype(sums.dtype)
        for at in range(c * chunk // block, (c + 1) * chunk // block):
            for side in range(2):
                step = side * n_expert + at
                if at == n_expert:
                    locals_.append(
                        local_copy(7 + side, sums.at[pl.ds(side * part + main, block)], rest_out.at[pl.ds(side * block, block)])
                    )
                elif step == 0:
                    locals_.append(local_copy(6, sums.at[lines_of(0)], back_ref.at[mine]))
                else:
                    copy = pltpu.make_async_remote_copy(
                        src_ref=sums.at[lines_of(step)],
                        dst_ref=back_ref.at[mine],
                        send_sem=back_send.at[step],
                        recv_sem=back_recv.at[step],
                        device_id=behind(step),
                        device_id_type=MESH,
                    )
                    copy.start()
                    returns.append(copy)
    for copy in locals_:
        copy.wait()
    for copy in returns:
        copy.wait()
    for copy in spread + sent:
        copy.wait_send()


def expert_exchange(blocks, rest, gates, ups, downs, collective_id):
    n_expert, block, width = blocks.shape
    peers = Z_HALVES * n_expert
    ff = gates[0].shape[1]
    bf16 = jnp.bfloat16
    count = peers * block + rest.shape[0]
    anywhere = pl.BlockSpec(memory_space=pl.ANY)
    sends = 2 * (peers + 2) + 8 * CHUNKS
    return pl.pallas_call(
        expert_kernel,
        out_shape=(
            jax.ShapeDtypeStruct((peers, block, width), bf16),
            jax.ShapeDtypeStruct(rest.shape, bf16),
        ),
        in_specs=[anywhere] * 8,
        out_specs=(anywhere, anywhere),
        scratch_shapes=[
            pltpu.VMEM((count, width), bf16),
            pltpu.VMEM((3, count, width), bf16),
            pltpu.VMEM((4, count, width), bf16),
            pltpu.VMEM((2, count, width), bf16),
            pltpu.VMEM((count, width), bf16),
            pltpu.VMEM((count, width), bf16),
            pltpu.VMEM((2, count, ff), bf16),
            pltpu.VMEM((2, width, ff), bf16),
            pltpu.VMEM((2, width, ff), bf16),
            pltpu.VMEM((2, ff, width), bf16),
            pltpu.SemaphoreType.DMA((peers,)),
            pltpu.SemaphoreType.DMA((peers,)),
            pltpu.SemaphoreType.DMA((peers,)),
            pltpu.SemaphoreType.DMA((peers,)),
            pltpu.SemaphoreType.DMA((sends,)),
            pltpu.SemaphoreType.DMA((sends,)),
            pltpu.SemaphoreType.DMA((9,)),
        ],
        compiler_params=pltpu.CompilerParams(
            collective_id=collective_id, has_side_effects=True, vmem_limit_bytes=66 * 1024 * 1000 - 560000
        ),
        name="expert_exchange",
    )(blocks, rest, *gates, *ups, *downs)


def local(
    pre_hidden,
    dec_resid,
    dec_query,
    kv_pool,
    page_table,
    cache_len,
    out_weight,
    norm_gain,
    route_ids_pre,
    route_ids_dec,
    route_logit_pre,
    route_logit_dec,
    expert_slot,
    w_gate,
    w_up,
    w_down,
):
    n_expert = lax.axis_size("expert")
    n_shard = lax.axis_size("shard")
    swap = [(at, at ^ 1) for at in range(n_shard)]
    gates = (w_gate[0], lax.ppermute(w_gate[0], "shard", swap))
    ups = (w_up[0], lax.ppermute(w_up[0], "shard", swap))
    downs = (w_down[0], lax.ppermute(w_down[0], "shard", swap))
    attn = pool_attention(dec_query, kv_pool, page_table[0], cache_len[0])
    head_part = jnp.dot(attn, out_weight, preferred_element_type=jnp.float32).astype(jnp.bfloat16)
    head_parts = lax.all_to_all(
        head_part.reshape(n_expert, -1, head_part.shape[1]), "expert", split_axis=0, concat_axis=0, tiled=True
    )
    head_total = jnp.sum(head_parts.astype(jnp.float32), axis=0)
    h_dec = (dec_resid[0].astype(jnp.float32) + head_total).astype(jnp.bfloat16)
    hidden = jnp.concatenate([pre_hidden, h_dec], axis=0)
    route_ids = jnp.concatenate([route_ids_pre, route_ids_dec[0]], axis=0)
    logits = jnp.concatenate([route_logit_pre, route_logit_dec[0]], axis=0)
    pre_count = pre_hidden.shape[0]
    rows_dev, width = hidden.shape
    slot_cap = (rows_dev + 3) // 4 + 2
    stream = hidden.astype(jnp.float32)
    normed = (
        stream * lax.rsqrt(jnp.mean(stream * stream, axis=-1, keepdims=True) + 1e-05) * norm_gain
    ).astype(jnp.bfloat16)
    shares = jnp.stack(
        [jax.nn.sigmoid(logits[:, 0] - logits[:, 1]), jax.nn.sigmoid(logits[:, 1] - logits[:, 0])],
        axis=-1,
    )
    experts = expert_slot.shape[0]
    expert_ids = jnp.arange(experts, dtype=jnp.int32)
    slot_match = expert_slot[None, :] == expert_ids[:, None]
    slot_of = jnp.sum(jnp.where(slot_match, expert_ids[None, :], 0), axis=1)
    slot_ids = jnp.sum(jnp.where(route_ids[..., None] == expert_ids, slot_of, 0), axis=-1)
    flat_slots = slot_ids.reshape(-1)
    slot_hot = (flat_slots[:, None] == expert_ids[None, :]).astype(jnp.int32)
    ranking = jnp.sum((jnp.cumsum(slot_hot, axis=0) - slot_hot) * slot_hot, axis=1)
    rest_cap = slot_cap - BLOCK
    main_all = experts * BLOCK
    slots_all = experts * slot_cap
    slot_pos = jnp.where(
        ranking < BLOCK, flat_slots * BLOCK + ranking, main_all + flat_slots * rest_cap + ranking - BLOCK
    ).reshape(rows_dev, 2)
    chosen = jnp.arange(slots_all, dtype=jnp.int32)[:, None, None] == slot_pos[None]
    placing = jnp.any(chosen, axis=-1).astype(jnp.bfloat16)
    lanes = 128
    blocks = jnp.dot(placing[:main_all], normed, preferred_element_type=jnp.float32).astype(jnp.bfloat16)
    rest = jnp.dot(placing[main_all:], normed, preferred_element_type=jnp.float32).astype(jnp.bfloat16)
    rest_in = plane_exchange(
        rest.reshape(experts, rest_cap, width // lanes, lanes), n_expert, False, 0
    ).reshape(-1, width)
    back, rest_sums = expert_exchange(
        blocks.reshape(experts, BLOCK, width), rest_in, gates, ups, downs, 1
    )
    rest_back = plane_exchange(
        rest_sums.reshape(Z_HALVES * n_expert, rest_cap, width // lanes, lanes), n_expert, True, 2
    ).reshape(Z_HALVES, experts * rest_cap, width)
    back = back.reshape(Z_HALVES, main_all, width)
    picking = (slot_pos.T.reshape(-1)[:, None] == jnp.arange(slots_all, dtype=jnp.int32)[None, :]).astype(
        jnp.bfloat16
    )

    def pick(mask, halves):
        outputs = (halves[0].astype(jnp.float32) + halves[1].astype(jnp.float32)).astype(jnp.bfloat16)
        return jnp.dot(mask, outputs, preferred_element_type=jnp.float32)

    picked = (pick(picking[:, :main_all], back) + pick(picking[:, main_all:], rest_back)).reshape(
        2, rows_dev, width
    )
    mixed_rows = stream + shares[:, :1] * picked[0] + shares[:, 1:] * picked[1]
    mixed_out = mixed_rows.astype(jnp.bfloat16)
    return (mixed_out[:pre_count], mixed_out[pre_count:][None])


def solution(mesh):
    placed = (
        P(("expert", "shard"), None),
        P("shard", "expert", None),
        P("shard", "expert"),
        P("expert", "shard", None, None),
        P("shard", None, None),
        P("shard", None),
        P("expert", None),
        P(),
        P(("expert", "shard"), None),
        P("shard", "expert", None),
        P(("expert", "shard"), None),
        P("shard", "expert", None),
        P(),
        P("expert", None, "shard"),
        P("expert", None, "shard"),
        P("expert", "shard", None),
    )
    return jax.shard_map(
        local,
        mesh=mesh,
        in_specs=placed,
        out_specs=(P(("expert", "shard"), None), P("shard", "expert", None)),
        check_vma=False,
    )
```

```python
import jax
import jax.numpy as jnp
from jax import lax
from jax.experimental import pallas as pl
from jax.experimental.pallas import tpu as pltpu
from jax.sharding import PartitionSpec as P

MESH = pl.DeviceIdType.MESH
X_CHIPS = 4
CORES = 2
Z_HALVES = 2
SHARD_PLANE = X_CHIPS * CORES
LOWEST = -1e30
BLOCK = 16
CHUNKS = 3


def attention_kernel(q_ref, count_ref, kv_ref, out_ref, top, total, summed):
    step = pl.program_id(0)

    @pl.when(step == 0)
    def _():
        top[...] = jnp.full(top.shape, LOWEST, jnp.float32)
        total[...] = jnp.zeros(total.shape, jnp.float32)
        summed[...] = jnp.zeros(summed.shape, jnp.float32)

    head_dim = q_ref.shape[1]
    positions = kv_ref.shape[0]
    pages = count_ref.shape[2]
    page_size = positions // pages
    scores = lax.dot_general(
        q_ref[...], kv_ref[:, :head_dim], (((1,), (1,)), ((), ())), preferred_element_type=jnp.float32
    ) * head_dim ** (-0.5)
    page_of = lax.broadcasted_iota(jnp.int32, (pages, positions), 1) // page_size
    spread = (page_of == lax.broadcasted_iota(jnp.int32, (pages, positions), 0)).astype(jnp.bfloat16)
    counts = jnp.dot(count_ref[0], spread, preferred_element_type=jnp.float32)
    offset = (lax.broadcasted_iota(jnp.int32, (1, positions), 1) % page_size).astype(jnp.float32)
    live = counts > offset
    scores = jnp.where(live, scores, LOWEST)
    new_top = jnp.maximum(top[...], jnp.max(scores, axis=1, keepdims=True))
    scale = jnp.exp(top[...] - new_top)
    weights = jnp.where(live, jnp.exp(scores - new_top), 0.0)
    top[...] = new_top
    total[...] = total[...] * scale + jnp.sum(weights, axis=1, keepdims=True)
    summed[...] = summed[...] * scale + jnp.dot(
        weights.astype(jnp.bfloat16), kv_ref[:, head_dim:], preferred_element_type=jnp.float32
    )

    @pl.when(step == pl.num_programs(0) - 1)
    def _():
        out_ref[...] = (summed[...] / total[...]).astype(out_ref.dtype)


def pool_attention(dec_query, kv_pool, page_rows, lengths):
    dec_dev, local_cols = dec_query.shape
    _, pool_dev, page_size, twice_dim = kv_pool.shape
    head_dim = twice_dim // 2
    group = local_cols // head_dim
    max_pages = page_rows.shape[1]
    steps = 16
    pages = pool_dev // steps
    in_page = jnp.clip(
        lengths[:, None] - page_size * jnp.arange(max_pages, dtype=jnp.int32)[None, :], 0, page_size
    )
    pool_ids = jnp.arange(pool_dev, dtype=jnp.int32)
    counts = jnp.sum(
        jnp.where(page_rows[:, :, None] == pool_ids[None, None, :], in_page[:, :, None], 0), axis=1
    ).astype(jnp.bfloat16)
    counts = jnp.repeat(counts, group, axis=0).reshape(dec_dev * group, steps, pages).transpose(1, 0, 2)
    rows = dec_dev * group
    return pl.pallas_call(
        attention_kernel,
        grid=(steps,),
        in_specs=[
            pl.BlockSpec((rows, head_dim), lambda i: (0, 0)),
            pl.BlockSpec((1, rows, pages), lambda i: (i, 0, 0)),
            pl.BlockSpec((pages * page_size, twice_dim), lambda i: (i, 0)),
        ],
        out_specs=pl.BlockSpec((rows, head_dim), lambda i: (0, 0)),
        out_shape=jax.ShapeDtypeStruct((rows, head_dim), jnp.bfloat16),
        scratch_shapes=[
            pltpu.VMEM((rows, 1), jnp.float32),
            pltpu.VMEM((rows, 1), jnp.float32),
            pltpu.VMEM((rows, head_dim), jnp.float32),
        ],
        cost_estimate=pl.CostEstimate(
            flops=4 * rows * head_dim * pool_dev * page_size,
            bytes_accessed=pool_dev * page_size * twice_dim * 2,
            transcendentals=rows * pool_dev * page_size,
        ),
        name="pool_attention",
    )(dec_query.reshape(rows, head_dim), counts, kv_pool.reshape(pool_dev * page_size, twice_dim)).reshape(
        dec_dev, local_cols
    )


def expert_kernel(
    blocks_ref, rest_ref, gate0, gate1, up0, up1, down0, down1, back_ref, rest_out,
    rows, held, partial, direct, relayed, sums, act, gate, up, down, rest_in, rest_sums, unpacked,
    plane_send, plane_recv, back_send, back_recv, rest_send, rest_recv, over_send, over_recv,
    send_sem, recv_sem, load_sem,
):
    expert = lax.axis_index("expert")
    shard = lax.axis_index("shard")
    n_expert, block, width = blocks_ref.shape
    half, rest = shard // SHARD_PLANE, shard % SHARD_PLANE
    chip, core = rest // CORES, rest % CORES
    right = half * SHARD_PLANE + (chip + 1) % X_CHIPS * CORES + core
    left = half * SHARD_PLANE + (chip + X_CHIPS - 1) % X_CHIPS * CORES + core
    mine = half * n_expert + expert
    peers = Z_HALVES * n_expert
    count = rows.shape[0]
    part = count // 2
    chunk = part // CHUNKS
    main = n_expert * block

    def ahead(step):
        to_half = (half + step // n_expert) % Z_HALVES
        return (expert + step) % n_expert, to_half * SHARD_PLANE + rest

    def behind(step):
        to_half = (half + step // n_expert) % Z_HALVES
        return (expert + n_expert - step % n_expert) % n_expert, to_half * SHARD_PLANE + rest

    def lines_of(step):
        return pl.ds(step // n_expert * part + step % n_expert * block, block)

    def local_copy(at, src, dst):
        copy = pltpu.make_async_copy(src, dst, load_sem.at[at])
        copy.start()
        return copy

    own = local_copy(6, blocks_ref.at[expert], rows.at[lines_of(0)])
    own_rest = local_copy(7, rest_ref.at[expert], rest_in.at[0])
    loads = [
        local_copy(at, src, dst)
        for at, (src, dst) in enumerate(
            ((gate0, gate.at[0]), (up0, up.at[0]), (gate1, gate.at[1]), (up1, up.at[1]), (down0, down.at[0]), (down1, down.at[1]))
        )
    ]

    barrier = pltpu.get_barrier_semaphore()
    for neighbour in (left, right):
        pl.semaphore_signal(barrier, inc=1, device_id=(expert, neighbour), device_id_type=MESH)
    for step in range(1, peers):
        pl.semaphore_signal(barrier, inc=1, device_id=ahead(step), device_id_type=MESH)
    pl.semaphore_wait(barrier, peers + 1)

    over = rest_ref.shape[1]
    spread_rest = []
    for step in range(1, peers):
        copy = pltpu.make_async_remote_copy(
            src_ref=rest_ref.at[ahead(step)[0]],
            dst_ref=rest_in.at[step],
            send_sem=rest_send.at[step],
            recv_sem=rest_recv.at[step],
            device_id=ahead(step),
            device_id_type=MESH,
        )
        copy.start()
        spread_rest.append(copy)
    spread = []
    for step in range(1, peers):
        copy = pltpu.make_async_remote_copy(
            src_ref=blocks_ref.at[ahead(step)[0]],
            dst_ref=rows.at[lines_of(step)],
            send_sem=plane_send.at[step],
            recv_sem=plane_recv.at[step],
            device_id=ahead(step),
            device_id_type=MESH,
        )
        copy.start()
        spread.append(copy)

    sent = []

    def send(src, dst, to):
        at = len(sent)
        copy = pltpu.make_async_remote_copy(
            src_ref=src,
            dst_ref=dst,
            send_sem=send_sem.at[at],
            recv_sem=recv_sem.at[at],
            device_id=(expert, to),
            device_id_type=MESH,
        )
        copy.start()
        sent.append(copy)
        return copy

    near = [[], []]
    later = []

    def forward(lines, side):
        near[side].append(send(rows.at[lines], held.at[side, lines], right))
        later.append(send(rows.at[lines], held.at[1 - side, lines], left))

    own.wait()
    forward(lines_of(0), 0)
    for step in range(1, peers):
        spread[step - 1].wait_recv()
        forward(lines_of(step), step // n_expert)
        if step == n_expert // 2:
            own_rest.wait()
            for copy in spread_rest:
                copy.wait_recv()
            for at in range(peers):
                unpacked[pl.ds(at * over, over), :] = rest_in[at].astype(jnp.float32)
            for side in range(2):
                rows[pl.ds(side * part + main, block), :] = unpacked[pl.ds(side * block, block), :].astype(rows.dtype)
                forward(pl.ds(side * part + main, block), side)
    for load in loads:
        load.wait()

    ff = gate.shape[2]
    tile = 256
    wide = 512

    def feed_forward(src, dst):
        for side in range(2):
            @pl.loop(0, ff // tile)
            def _(t):
                columns = pl.ds(pl.multiple_of(t * tile, tile), tile)
                g = jnp.dot(src[...], gate[side, :, columns], preferred_element_type=jnp.float32)
                u = jnp.dot(src[...], up[side, :, columns], preferred_element_type=jnp.float32)
                act[side, :, columns] = (g / (1.0 + jnp.exp(-g)) * u).astype(act.dtype)

        @pl.loop(0, width // wide)
        def _(t):
            columns = pl.ds(pl.multiple_of(t * wide, wide), wide)
            o = jnp.dot(act[0], down[0, :, columns], preferred_element_type=jnp.float32)
            o = o + jnp.dot(act[1], down[1, :, columns], preferred_element_type=jnp.float32)
            dst[:, columns] = o.astype(dst.dtype)

    def piece(side, c):
        return pl.ds(side * part + c * chunk, chunk)

    feed_forward(rows, partial.at[3])
    for copy in near[0] + near[1] + later:
        copy.wait_recv()
    third = []
    for c in range(CHUNKS):
        third.append(send(held.at[0, piece(0, c)], held.at[2, piece(0, c)], right))
        third.append(send(held.at[0, piece(1, c)], held.at[2, piece(1, c)], left))
    feed_forward(held.at[0], partial.at[0])

    def send_plain(c):
        return (
            send(partial.at[0, piece(1, c)], direct.at[0, piece(1, c)], right),
            send(partial.at[0, piece(0, c)], direct.at[1, piece(0, c)], left),
        )

    def send_far(c):
        return (
            send(partial.at[2, piece(0, c)], relayed.at[piece(0, c)], right),
            send(partial.at[2, piece(1, c)], relayed.at[piece(1, c)], left),
        )

    def send_joined(c, far):
        joined = []
        for side, to in ((0, right), (1, left)):
            far[side].wait_recv()
            lines = piece(side, c)
            partial[1, lines, :] = (
                partial[1, lines, :].astype(jnp.float32) + relayed[lines, :].astype(jnp.float32)
            ).astype(partial.dtype)
            joined.append(send(partial.at[1, lines], direct.at[side, lines], to))
        return joined

    plain = [send_plain(0), send_plain(1)]
    feed_forward(held.at[1], partial.at[1])
    for copy in third:
        copy.wait_recv()
    feed_forward(held.at[2], partial.at[2])
    far = [send_far(0), send_far(1)]
    joined = [send_joined(0, far[0])]
    far.append(send_far(2))
    joined.append(send_joined(1, far[1]))
    plain.append(send_plain(2))
    joined.append(send_joined(2, far[2]))

    returns = []
    locals_ = []
    for c in range(CHUNKS):
        for copy in (*plain[c], *joined[c]):
            copy.wait_recv()
        for side in range(2):
            lines = piece(side, c)
            sums[lines, :] = (
                partial[3, lines, :].astype(jnp.float32)
                + direct[0, lines, :].astype(jnp.float32)
                + direct[1, lines, :].astype(jnp.float32)
            ).astype(sums.dtype)
        for at in range(c * chunk // block, (c + 1) * chunk // block):
            for side in range(2):
                step = side * n_expert + at
                if at == n_expert:
                    unpacked[pl.ds(side * block, block), :] = sums[pl.ds(side * part + main, block), :].astype(jnp.float32)
                    for step in range(side * n_expert, (side + 1) * n_expert):
                        rest_sums[step] = unpacked[pl.ds(step * over, over), :].astype(rest_sums.dtype)
                    for step in range(side * n_expert, (side + 1) * n_expert):
                        if step == 0:
                            locals_.append(local_copy(7, rest_sums.at[0], rest_out.at[mine]))
                            continue
                        copy = pltpu.make_async_remote_copy(
                            src_ref=rest_sums.at[step],
                            dst_ref=rest_out.at[mine],
                            send_sem=over_send.at[step],
                            recv_sem=over_recv.at[step],
                            device_id=behind(step),
                            device_id_type=MESH,
                        )
                        copy.start()
                        returns.append(copy)
                elif step == 0:
                    locals_.append(local_copy(6, sums.at[lines_of(0)], back_ref.at[mine]))
                else:
                    copy = pltpu.make_async_remote_copy(
                        src_ref=sums.at[lines_of(step)],
                        dst_ref=back_ref.at[mine],
                        send_sem=back_send.at[step],
                        recv_sem=back_recv.at[step],
                        device_id=behind(step),
                        device_id_type=MESH,
                    )
                    copy.start()
                    returns.append(copy)
    for copy in locals_:
        copy.wait()
    for copy in returns:
        copy.wait()
    for copy in spread_rest + spread + sent:
        copy.wait_send()


def expert_exchange(blocks, rest, gates, ups, downs, collective_id):
    n_expert, block, width = blocks.shape
    peers = Z_HALVES * n_expert
    ff = gates[0].shape[1]
    bf16 = jnp.bfloat16
    over = rest.shape[1]
    count = peers * (block + over)
    anywhere = pl.BlockSpec(memory_space=pl.ANY)
    sends = 2 * (peers + 2) + 8 * CHUNKS
    return pl.pallas_call(
        expert_kernel,
        out_shape=(
            jax.ShapeDtypeStruct((peers, block, width), bf16),
            jax.ShapeDtypeStruct((peers, over, width), bf16),
        ),
        in_specs=[anywhere] * 8,
        out_specs=(anywhere, anywhere),
        scratch_shapes=[
            pltpu.VMEM((count, width), bf16),
            pltpu.VMEM((3, count, width), bf16),
            pltpu.VMEM((4, count, width), bf16),
            pltpu.VMEM((2, count, width), bf16),
            pltpu.VMEM((count, width), bf16),
            pltpu.VMEM((count, width), bf16),
            pltpu.VMEM((2, count, ff), bf16),
            pltpu.VMEM((2, width, ff), bf16),
            pltpu.VMEM((2, width, ff), bf16),
            pltpu.VMEM((2, ff, width), bf16),
            pltpu.VMEM((peers, over, width), bf16),
            pltpu.VMEM((peers, over, width), bf16),
            pltpu.VMEM((peers * over, width), jnp.float32),
            pltpu.SemaphoreType.DMA((peers,)),
            pltpu.SemaphoreType.DMA((peers,)),
            pltpu.SemaphoreType.DMA((peers,)),
            pltpu.SemaphoreType.DMA((peers,)),
            pltpu.SemaphoreType.DMA((peers,)),
            pltpu.SemaphoreType.DMA((peers,)),
            pltpu.SemaphoreType.DMA((peers,)),
            pltpu.SemaphoreType.DMA((peers,)),
            pltpu.SemaphoreType.DMA((sends,)),
            pltpu.SemaphoreType.DMA((sends,)),
            pltpu.SemaphoreType.DMA((8,)),
        ],
        compiler_params=pltpu.CompilerParams(
            collective_id=collective_id, has_side_effects=True, vmem_limit_bytes=66 * 1024 * 1000 - 560000
        ),
        name="expert_exchange",
    )(blocks, rest, *gates, *ups, *downs)


def local(
    pre_hidden,
    dec_resid,
    dec_query,
    kv_pool,
    page_table,
    cache_len,
    out_weight,
    norm_gain,
    route_ids_pre,
    route_ids_dec,
    route_logit_pre,
    route_logit_dec,
    expert_slot,
    w_gate,
    w_up,
    w_down,
):
    n_expert = lax.axis_size("expert")
    n_shard = lax.axis_size("shard")
    swap = [(at, at ^ 1) for at in range(n_shard)]
    gates = (w_gate[0], lax.ppermute(w_gate[0], "shard", swap))
    ups = (w_up[0], lax.ppermute(w_up[0], "shard", swap))
    downs = (w_down[0], lax.ppermute(w_down[0], "shard", swap))
    attn = pool_attention(dec_query, kv_pool, page_table[0], cache_len[0])
    head_part = jnp.dot(attn, out_weight, preferred_element_type=jnp.float32).astype(jnp.bfloat16)
    head_parts = lax.all_to_all(
        head_part.reshape(n_expert, -1, head_part.shape[1]), "expert", split_axis=0, concat_axis=0, tiled=True
    )
    head_total = jnp.sum(head_parts.astype(jnp.float32), axis=0)
    h_dec = (dec_resid[0].astype(jnp.float32) + head_total).astype(jnp.bfloat16)
    hidden = jnp.concatenate([pre_hidden, h_dec], axis=0)
    route_ids = jnp.concatenate([route_ids_pre, route_ids_dec[0]], axis=0)
    logits = jnp.concatenate([route_logit_pre, route_logit_dec[0]], axis=0)
    pre_count = pre_hidden.shape[0]
    rows_dev, width = hidden.shape
    slot_cap = (rows_dev + 3) // 4 + 2
    stream = hidden.astype(jnp.float32)
    normed = (
        stream * lax.rsqrt(jnp.mean(stream * stream, axis=-1, keepdims=True) + 1e-05) * norm_gain
    ).astype(jnp.bfloat16)
    shares = jnp.stack(
        [jax.nn.sigmoid(logits[:, 0] - logits[:, 1]), jax.nn.sigmoid(logits[:, 1] - logits[:, 0])],
        axis=-1,
    )
    experts = expert_slot.shape[0]
    expert_ids = jnp.arange(experts, dtype=jnp.int32)
    slot_match = expert_slot[None, :] == expert_ids[:, None]
    slot_of = jnp.sum(jnp.where(slot_match, expert_ids[None, :], 0), axis=1)
    slot_ids = jnp.sum(jnp.where(route_ids[..., None] == expert_ids, slot_of, 0), axis=-1)
    flat_slots = slot_ids.reshape(-1)
    slot_hot = (flat_slots[:, None] == expert_ids[None, :]).astype(jnp.int32)
    ranking = jnp.sum((jnp.cumsum(slot_hot, axis=0) - slot_hot) * slot_hot, axis=1)
    rest_cap = slot_cap - BLOCK
    main_all = experts * BLOCK
    slots_all = experts * slot_cap
    slot_pos = jnp.where(
        ranking < BLOCK, flat_slots * BLOCK + ranking, main_all + flat_slots * rest_cap + ranking - BLOCK
    ).reshape(rows_dev, 2)
    chosen = jnp.arange(slots_all, dtype=jnp.int32)[:, None, None] == slot_pos[None]
    placing = jnp.any(chosen, axis=-1).astype(jnp.bfloat16)
    blocks = jnp.dot(placing[:main_all], normed, preferred_element_type=jnp.float32).astype(jnp.bfloat16)
    rest = jnp.dot(placing[main_all:], normed, preferred_element_type=jnp.float32).astype(jnp.bfloat16)
    back, rest_back = expert_exchange(
        blocks.reshape(experts, BLOCK, width), rest.reshape(experts, rest_cap, width), gates, ups, downs, 0
    )
    rest_back = rest_back.reshape(Z_HALVES, experts * rest_cap, width)
    back = back.reshape(Z_HALVES, main_all, width)
    picking = (slot_pos.T.reshape(-1)[:, None] == jnp.arange(slots_all, dtype=jnp.int32)[None, :]).astype(
        jnp.bfloat16
    )

    def pick(mask, halves):
        outputs = (halves[0].astype(jnp.float32) + halves[1].astype(jnp.float32)).astype(jnp.bfloat16)
        return jnp.dot(mask, outputs, preferred_element_type=jnp.float32)

    picked = (pick(picking[:, :main_all], back) + pick(picking[:, main_all:], rest_back)).reshape(
        2, rows_dev, width
    )
    mixed_rows = stream + shares[:, :1] * picked[0] + shares[:, 1:] * picked[1]
    mixed_out = mixed_rows.astype(jnp.bfloat16)
    return (mixed_out[:pre_count], mixed_out[pre_count:][None])


def solution(mesh):
    placed = (
        P(("expert", "shard"), None),
        P("shard", "expert", None),
        P("shard", "expert"),
        P("expert", "shard", None, None),
        P("shard", None, None),
        P("shard", None),
        P("expert", None),
        P(),
        P(("expert", "shard"), None),
        P("shard", "expert", None),
        P(("expert", "shard"), None),
        P("shard", "expert", None),
        P(),
        P("expert", None, "shard"),
        P("expert", None, "shard"),
        P("expert", "shard", None),
    )
    return jax.shard_map(
        local,
        mesh=mesh,
        in_specs=placed,
        out_specs=(P(("expert", "shard"), None), P("shard", "expert", None)),
        check_vma=False,
    )
```

```python
import jax
import jax.numpy as jnp
from jax import lax
from jax.experimental import pallas as pl
from jax.experimental.pallas import tpu as pltpu
from jax.sharding import PartitionSpec as P

MESH = pl.DeviceIdType.MESH
X_CHIPS = 4
CORES = 2
Z_HALVES = 2
SHARD_PLANE = X_CHIPS * CORES
LOWEST = -1e30
BLOCK = 16
CHUNKS = 3


def attention_kernel(q_ref, count_ref, kv_ref, out_ref, top, total, summed, spread, offset):
    step = pl.program_id(0)
    head_dim = q_ref.shape[1]
    pages, positions = spread.shape
    page_size = positions // pages

    @pl.when(step == 0)
    def _():
        top[...] = jnp.full(top.shape, LOWEST, jnp.float32)
        total[...] = jnp.zeros(total.shape, jnp.float32)
        summed[...] = jnp.zeros(summed.shape, jnp.float32)
        page_of = lax.broadcasted_iota(jnp.int32, (pages, positions), 1) // page_size
        spread[...] = (page_of == lax.broadcasted_iota(jnp.int32, (pages, positions), 0)).astype(spread.dtype)
        offset[...] = (lax.broadcasted_iota(jnp.int32, (1, positions), 1) % page_size).astype(jnp.float32)

    scores = lax.dot_general(
        q_ref[...], kv_ref[:, :head_dim], (((1,), (1,)), ((), ())), preferred_element_type=jnp.float32
    ) * head_dim ** (-0.5)
    counts = jnp.dot(count_ref[0], spread[...], preferred_element_type=jnp.float32)
    live = counts > offset[...]
    scores = jnp.where(live, scores, LOWEST)
    new_top = jnp.maximum(top[...], jnp.max(scores, axis=1, keepdims=True))
    scale = jnp.exp(top[...] - new_top)
    weights = jnp.where(live, jnp.exp(scores - new_top), 0.0)
    top[...] = new_top
    total[...] = total[...] * scale + jnp.sum(weights, axis=1, keepdims=True)
    summed[...] = summed[...] * scale + jnp.dot(
        weights.astype(jnp.bfloat16), kv_ref[:, head_dim:], preferred_element_type=jnp.float32
    )

    @pl.when(step == pl.num_programs(0) - 1)
    def _():
        out_ref[...] = (summed[...] / total[...]).astype(out_ref.dtype)


def pool_attention(dec_query, kv_pool, page_rows, lengths):
    dec_dev, local_cols = dec_query.shape
    _, pool_dev, page_size, twice_dim = kv_pool.shape
    head_dim = twice_dim // 2
    group = local_cols // head_dim
    max_pages = page_rows.shape[1]
    steps = 6
    pages = pool_dev // steps
    in_page = jnp.clip(
        lengths[:, None] - page_size * jnp.arange(max_pages, dtype=jnp.int32)[None, :], 0, page_size
    )
    pool_ids = jnp.arange(pool_dev, dtype=jnp.int32)
    counts = jnp.sum(
        jnp.where(page_rows[:, :, None] == pool_ids[None, None, :], in_page[:, :, None], 0), axis=1
    ).astype(jnp.bfloat16)
    counts = jnp.repeat(counts, group, axis=0).reshape(dec_dev * group, steps, pages).transpose(1, 0, 2)
    rows = dec_dev * group
    return pl.pallas_call(
        attention_kernel,
        grid=(steps,),
        in_specs=[
            pl.BlockSpec((rows, head_dim), lambda i: (0, 0)),
            pl.BlockSpec((1, rows, pages), lambda i: (i, 0, 0)),
            pl.BlockSpec((pages * page_size, twice_dim), lambda i: (i, 0)),
        ],
        out_specs=pl.BlockSpec((rows, head_dim), lambda i: (0, 0)),
        out_shape=jax.ShapeDtypeStruct((rows, head_dim), jnp.bfloat16),
        scratch_shapes=[
            pltpu.VMEM((rows, 1), jnp.float32),
            pltpu.VMEM((rows, 1), jnp.float32),
            pltpu.VMEM((rows, head_dim), jnp.float32),
            pltpu.VMEM((pages, pages * page_size), jnp.bfloat16),
            pltpu.VMEM((1, pages * page_size), jnp.float32),
        ],
        cost_estimate=pl.CostEstimate(
            flops=4 * rows * head_dim * pool_dev * page_size,
            bytes_accessed=pool_dev * page_size * twice_dim * 2,
            transcendentals=rows * pool_dev * page_size,
        ),
        name="pool_attention",
    )(dec_query.reshape(rows, head_dim), counts, kv_pool.reshape(pool_dev * page_size, twice_dim)).reshape(
        dec_dev, local_cols
    )


def expert_kernel(
    blocks_ref, rest_ref, gate0, gate1, up0, up1, down0, down1, back_ref, rest_out,
    rows, held, partial, direct, relayed, sums, act, gate, up, down, rest_in, rest_sums, unpacked,
    plane_send, plane_recv, back_send, back_recv, rest_send, rest_recv, over_send, over_recv,
    send_sem, recv_sem, load_sem,
):
    expert = lax.axis_index("expert")
    shard = lax.axis_index("shard")
    n_expert, block, width = blocks_ref.shape
    half, rest = shard // SHARD_PLANE, shard % SHARD_PLANE
    chip, core = rest // CORES, rest % CORES
    right = half * SHARD_PLANE + (chip + 1) % X_CHIPS * CORES + core
    left = half * SHARD_PLANE + (chip + X_CHIPS - 1) % X_CHIPS * CORES + core
    mine = half * n_expert + expert
    peers = Z_HALVES * n_expert
    count = rows.shape[0]
    part = count // 2
    chunk = part // CHUNKS
    main = n_expert * block

    def ahead(step):
        to_half = (half + step // n_expert) % Z_HALVES
        return (expert + step) % n_expert, to_half * SHARD_PLANE + rest

    def behind(step):
        to_half = (half + step // n_expert) % Z_HALVES
        return (expert + n_expert - step % n_expert) % n_expert, to_half * SHARD_PLANE + rest

    def lines_of(step):
        return pl.ds(step // n_expert * part + step % n_expert * block, block)

    def local_copy(at, src, dst):
        copy = pltpu.make_async_copy(src, dst, load_sem.at[at])
        copy.start()
        return copy

    own = local_copy(6, blocks_ref.at[expert], rows.at[lines_of(0)])
    own_rest = local_copy(7, rest_ref.at[expert], rest_in.at[0])
    loads = [
        local_copy(at, src, dst)
        for at, (src, dst) in enumerate(
            ((gate0, gate.at[0]), (up0, up.at[0]), (gate1, gate.at[1]), (up1, up.at[1]), (down0, down.at[0]), (down1, down.at[1]))
        )
    ]

    barrier = pltpu.get_barrier_semaphore()
    for neighbour in (left, right):
        pl.semaphore_signal(barrier, inc=1, device_id=(expert, neighbour), device_id_type=MESH)
    for step in range(1, peers):
        pl.semaphore_signal(barrier, inc=1, device_id=ahead(step), device_id_type=MESH)
    pl.semaphore_wait(barrier, peers + 1)

    over = rest_ref.shape[1]
    spread_rest = []
    for step in range(1, peers):
        copy = pltpu.make_async_remote_copy(
            src_ref=rest_ref.at[ahead(step)[0]],
            dst_ref=rest_in.at[step],
            send_sem=rest_send.at[step],
            recv_sem=rest_recv.at[step],
            device_id=ahead(step),
            device_id_type=MESH,
        )
        copy.start()
        spread_rest.append(copy)
    spread = []
    for step in range(1, peers):
        copy = pltpu.make_async_remote_copy(
            src_ref=blocks_ref.at[ahead(step)[0]],
            dst_ref=rows.at[lines_of(step)],
            send_sem=plane_send.at[step],
            recv_sem=plane_recv.at[step],
            device_id=ahead(step),
            device_id_type=MESH,
        )
        copy.start()
        spread.append(copy)

    sent = []

    def send(src, dst, to):
        at = len(sent)
        copy = pltpu.make_async_remote_copy(
            src_ref=src,
            dst_ref=dst,
            send_sem=send_sem.at[at],
            recv_sem=recv_sem.at[at],
            device_id=(expert, to),
            device_id_type=MESH,
        )
        copy.start()
        sent.append(copy)
        return copy

    near = [[], []]
    later = []

    def forward(lines, side):
        near[side].append(send(rows.at[lines], held.at[side, lines], right))
        later.append(send(rows.at[lines], held.at[1 - side, lines], left))

    own.wait()
    forward(lines_of(0), 0)
    for step in range(1, peers):
        spread[step - 1].wait_recv()
        forward(lines_of(step), step // n_expert)
        if step == n_expert // 2:
            own_rest.wait()
            for copy in spread_rest:
                copy.wait_recv()
            for at in range(peers):
                unpacked[pl.ds(at * over, over), :] = rest_in[at].astype(jnp.float32)
            for side in range(2):
                rows[pl.ds(side * part + main, block), :] = unpacked[pl.ds(side * block, block), :].astype(rows.dtype)
                forward(pl.ds(side * part + main, block), side)
    for load in loads:
        load.wait()

    ff = gate.shape[2]
    tile = 256
    wide = 512

    def feed_forward(src, dst):
        for side in range(2):
            @pl.loop(0, ff // tile)
            def _(t):
                columns = pl.ds(pl.multiple_of(t * tile, tile), tile)
                g = jnp.dot(src[...], gate[side, :, columns], preferred_element_type=jnp.float32)
                u = jnp.dot(src[...], up[side, :, columns], preferred_element_type=jnp.float32)
                act[side, :, columns] = (g / (1.0 + jnp.exp(-g)) * u).astype(act.dtype)

        @pl.loop(0, width // wide)
        def _(t):
            columns = pl.ds(pl.multiple_of(t * wide, wide), wide)
            o = jnp.dot(act[0], down[0, :, columns], preferred_element_type=jnp.float32)
            o = o + jnp.dot(act[1], down[1, :, columns], preferred_element_type=jnp.float32)
            dst[:, columns] = o.astype(dst.dtype)

    def piece(side, c):
        return pl.ds(side * part + c * chunk, chunk)

    feed_forward(rows, partial.at[3])
    for copy in near[0] + near[1] + later:
        copy.wait_recv()
    third = []
    for c in range(CHUNKS):
        third.append(send(held.at[0, piece(0, c)], held.at[2, piece(0, c)], right))
        third.append(send(held.at[0, piece(1, c)], held.at[2, piece(1, c)], left))
    feed_forward(held.at[0], partial.at[0])

    def send_plain(c):
        return (
            send(partial.at[0, piece(1, c)], direct.at[0, piece(1, c)], right),
            send(partial.at[0, piece(0, c)], direct.at[1, piece(0, c)], left),
        )

    def send_far(c):
        return (
            send(partial.at[2, piece(0, c)], relayed.at[piece(0, c)], right),
            send(partial.at[2, piece(1, c)], relayed.at[piece(1, c)], left),
        )

    def send_joined(c, far):
        joined = []
        for side, to in ((0, right), (1, left)):
            far[side].wait_recv()
            lines = piece(side, c)
            partial[1, lines, :] = (
                partial[1, lines, :].astype(jnp.float32) + relayed[lines, :].astype(jnp.float32)
            ).astype(partial.dtype)
            joined.append(send(partial.at[1, lines], direct.at[side, lines], to))
        return joined

    plain = [send_plain(0), send_plain(1)]
    feed_forward(held.at[1], partial.at[1])
    for copy in third:
        copy.wait_recv()
    feed_forward(held.at[2], partial.at[2])
    far = [send_far(0), send_far(1)]
    joined = [send_joined(0, far[0])]
    far.append(send_far(2))
    joined.append(send_joined(1, far[1]))
    plain.append(send_plain(2))
    joined.append(send_joined(2, far[2]))

    returns = []
    locals_ = []
    for c in range(CHUNKS):
        for copy in (*plain[c], *joined[c]):
            copy.wait_recv()
        for side in range(2):
            lines = piece(side, c)
            sums[lines, :] = (
                partial[3, lines, :].astype(jnp.float32)
                + direct[0, lines, :].astype(jnp.float32)
                + direct[1, lines, :].astype(jnp.float32)
            ).astype(sums.dtype)
        for at in range(c * chunk // block, (c + 1) * chunk // block):
            for side in range(2):
                step = side * n_expert + at
                if at == n_expert:
                    unpacked[pl.ds(side * block, block), :] = sums[pl.ds(side * part + main, block), :].astype(jnp.float32)
                    for step in range(side * n_expert, (side + 1) * n_expert):
                        rest_sums[step] = unpacked[pl.ds(step * over, over), :].astype(rest_sums.dtype)
                    for step in range(side * n_expert, (side + 1) * n_expert):
                        if step == 0:
                            locals_.append(local_copy(7, rest_sums.at[0], rest_out.at[mine]))
                            continue
                        copy = pltpu.make_async_remote_copy(
                            src_ref=rest_sums.at[step],
                            dst_ref=rest_out.at[mine],
                            send_sem=over_send.at[step],
                            recv_sem=over_recv.at[step],
                            device_id=behind(step),
                            device_id_type=MESH,
                        )
                        copy.start()
                        returns.append(copy)
                elif step == 0:
                    locals_.append(local_copy(6, sums.at[lines_of(0)], back_ref.at[mine]))
                else:
                    copy = pltpu.make_async_remote_copy(
                        src_ref=sums.at[lines_of(step)],
                        dst_ref=back_ref.at[mine],
                        send_sem=back_send.at[step],
                        recv_sem=back_recv.at[step],
                        device_id=behind(step),
                        device_id_type=MESH,
                    )
                    copy.start()
                    returns.append(copy)
    for copy in locals_:
        copy.wait()
    for copy in returns:
        copy.wait()
    for copy in spread_rest + spread + sent:
        copy.wait_send()


def expert_exchange(blocks, rest, gates, ups, downs, collective_id):
    n_expert, block, width = blocks.shape
    peers = Z_HALVES * n_expert
    ff = gates[0].shape[1]
    bf16 = jnp.bfloat16
    over = rest.shape[1]
    count = peers * (block + over)
    anywhere = pl.BlockSpec(memory_space=pl.ANY)
    sends = 2 * (peers + 2) + 8 * CHUNKS
    return pl.pallas_call(
        expert_kernel,
        out_shape=(
            jax.ShapeDtypeStruct((peers, block, width), bf16),
            jax.ShapeDtypeStruct((peers, over, width), bf16),
        ),
        in_specs=[anywhere] * 8,
        out_specs=(anywhere, anywhere),
        scratch_shapes=[
            pltpu.VMEM((count, width), bf16),
            pltpu.VMEM((3, count, width), bf16),
            pltpu.VMEM((4, count, width), bf16),
            pltpu.VMEM((2, count, width), bf16),
            pltpu.VMEM((count, width), bf16),
            pltpu.VMEM((count, width), bf16),
            pltpu.VMEM((2, count, ff), bf16),
            pltpu.VMEM((2, width, ff), bf16),
            pltpu.VMEM((2, width, ff), bf16),
            pltpu.VMEM((2, ff, width), bf16),
            pltpu.VMEM((peers, over, width), bf16),
            pltpu.VMEM((peers, over, width), bf16),
            pltpu.VMEM((peers * over, width), jnp.float32),
            pltpu.SemaphoreType.DMA((peers,)),
            pltpu.SemaphoreType.DMA((peers,)),
            pltpu.SemaphoreType.DMA((peers,)),
            pltpu.SemaphoreType.DMA((peers,)),
            pltpu.SemaphoreType.DMA((peers,)),
            pltpu.SemaphoreType.DMA((peers,)),
            pltpu.SemaphoreType.DMA((peers,)),
            pltpu.SemaphoreType.DMA((peers,)),
            pltpu.SemaphoreType.DMA((sends,)),
            pltpu.SemaphoreType.DMA((sends,)),
            pltpu.SemaphoreType.DMA((8,)),
        ],
        compiler_params=pltpu.CompilerParams(
            collective_id=collective_id, has_side_effects=True, vmem_limit_bytes=66 * 1024 * 1000 - 560000
        ),
        name="expert_exchange",
    )(blocks, rest, *gates, *ups, *downs)


def local(
    pre_hidden,
    dec_resid,
    dec_query,
    kv_pool,
    page_table,
    cache_len,
    out_weight,
    norm_gain,
    route_ids_pre,
    route_ids_dec,
    route_logit_pre,
    route_logit_dec,
    expert_slot,
    w_gate,
    w_up,
    w_down,
):
    n_expert = lax.axis_size("expert")
    n_shard = lax.axis_size("shard")
    swap = [(at, at ^ 1) for at in range(n_shard)]
    gates = (w_gate[0], lax.ppermute(w_gate[0], "shard", swap))
    ups = (w_up[0], lax.ppermute(w_up[0], "shard", swap))
    downs = (w_down[0], lax.ppermute(w_down[0], "shard", swap))
    attn = pool_attention(dec_query, kv_pool, page_table[0], cache_len[0])
    head_part = jnp.dot(attn, out_weight, preferred_element_type=jnp.float32).astype(jnp.bfloat16)
    head_parts = lax.all_to_all(
        head_part.reshape(n_expert, -1, head_part.shape[1]), "expert", split_axis=0, concat_axis=0, tiled=True
    )
    head_total = jnp.sum(head_parts.astype(jnp.float32), axis=0)
    h_dec = (dec_resid[0].astype(jnp.float32) + head_total).astype(jnp.bfloat16)
    hidden = jnp.concatenate([pre_hidden, h_dec], axis=0)
    route_ids = jnp.concatenate([route_ids_pre, route_ids_dec[0]], axis=0)
    logits = jnp.concatenate([route_logit_pre, route_logit_dec[0]], axis=0)
    pre_count = pre_hidden.shape[0]
    rows_dev, width = hidden.shape
    slot_cap = (rows_dev + 3) // 4 + 2
    stream = hidden.astype(jnp.float32)
    normed = (
        stream * lax.rsqrt(jnp.mean(stream * stream, axis=-1, keepdims=True) + 1e-05) * norm_gain
    ).astype(jnp.bfloat16)
    shares = jnp.stack(
        [jax.nn.sigmoid(logits[:, 0] - logits[:, 1]), jax.nn.sigmoid(logits[:, 1] - logits[:, 0])],
        axis=-1,
    )
    experts = expert_slot.shape[0]
    expert_ids = jnp.arange(experts, dtype=jnp.int32)
    slot_match = expert_slot[None, :] == expert_ids[:, None]
    slot_of = jnp.sum(jnp.where(slot_match, expert_ids[None, :], 0), axis=1)
    slot_ids = jnp.sum(jnp.where(route_ids[..., None] == expert_ids, slot_of, 0), axis=-1)
    flat_slots = slot_ids.reshape(-1)
    slot_hot = (flat_slots[:, None] == expert_ids[None, :]).astype(jnp.int32)
    ranking = jnp.sum((jnp.cumsum(slot_hot, axis=0) - slot_hot) * slot_hot, axis=1)
    rest_cap = slot_cap - BLOCK
    main_all = experts * BLOCK
    slots_all = experts * slot_cap
    slot_pos = jnp.where(
        ranking < BLOCK, flat_slots * BLOCK + ranking, main_all + flat_slots * rest_cap + ranking - BLOCK
    ).reshape(rows_dev, 2)
    chosen = jnp.arange(slots_all, dtype=jnp.int32)[:, None, None] == slot_pos[None]
    placing = jnp.any(chosen, axis=-1).astype(jnp.bfloat16)
    blocks = jnp.dot(placing[:main_all], normed, preferred_element_type=jnp.float32).astype(jnp.bfloat16)
    rest = jnp.dot(placing[main_all:], normed, preferred_element_type=jnp.float32).astype(jnp.bfloat16)
    back, rest_back = expert_exchange(
        blocks.reshape(experts, BLOCK, width), rest.reshape(experts, rest_cap, width), gates, ups, downs, 0
    )
    rest_back = rest_back.reshape(Z_HALVES, experts * rest_cap, width)
    back = back.reshape(Z_HALVES, main_all, width)
    picking = (slot_pos.T.reshape(-1)[:, None] == jnp.arange(slots_all, dtype=jnp.int32)[None, :]).astype(
        jnp.bfloat16
    )

    def pick(mask, halves):
        outputs = (halves[0].astype(jnp.float32) + halves[1].astype(jnp.float32)).astype(jnp.bfloat16)
        return jnp.dot(mask, outputs, preferred_element_type=jnp.float32)

    picked = (pick(picking[:, :main_all], back) + pick(picking[:, main_all:], rest_back)).reshape(
        2, rows_dev, width
    )
    mixed_rows = stream + shares[:, :1] * picked[0] + shares[:, 1:] * picked[1]
    mixed_out = mixed_rows.astype(jnp.bfloat16)
    return (mixed_out[:pre_count], mixed_out[pre_count:][None])


def solution(mesh):
    placed = (
        P(("expert", "shard"), None),
        P("shard", "expert", None),
        P("shard", "expert"),
        P("expert", "shard", None, None),
        P("shard", None, None),
        P("shard", None),
        P("expert", None),
        P(),
        P(("expert", "shard"), None),
        P("shard", "expert", None),
        P(("expert", "shard"), None),
        P("shard", "expert", None),
        P(),
        P("expert", None, "shard"),
        P("expert", None, "shard"),
        P("expert", "shard", None),
    )
    return jax.shard_map(
        local,
        mesh=mesh,
        in_specs=placed,
        out_specs=(P(("expert", "shard"), None), P("shard", "expert", None)),
        check_vma=False,
    )
```
